128 devices in a mesh: dp: 8 (over x, core), fsdp: 16 (over z, y).
Axes of the slice: x: 4, y: 4, z: 4, core: 2. Of those that a mesh axis runs over, the one named last changes fastest.
Arguments:
- tokens: bfloat16 [65536, 1408], P(('dp', 'fsdp')), may hold values from -6 to 6
- image_of: int32 [65536], P(('dp', 'fsdp')), may hold values from 0 to 16383, as said below
- live: int32 [65536], P(('dp', 'fsdp')), may hold values from 0 to 1, as said below
- request_of: int32 [16384], P('dp'), may hold values from -1 to 63, as said below
- ln1_gain: float32 [1408], replicated, may hold values from 0.5 to 1.5
- ln1_shift: float32 [1408], replicated, may hold values from -3 to 3
- w_qkv: bfloat16 [1408, 4224], P('fsdp')
- b_qkv: float32 [4224], replicated, may hold values from -3 to 3
- w_out: bfloat16 [1408, 1408], P('fsdp'), may hold values from -0.15625 to 0.15625
- b_out: float32 [1408], replicated, may hold values from -3 to 3
- ln2_gain: float32 [1408], replicated, may hold values from 0.5 to 1.5
- ln2_shift: float32 [1408], replicated, may hold values from -3 to 3
- w_proj: bfloat16 [5632, 4096], P(None, 'fsdp'), may hold values from -0.078125 to 0.078125
- b_proj: float32 [4096], P('fsdp'), may hold values from -3 to 3
Outputs:
- features: bfloat16 [16384, 4096], P('dp', 'fsdp')
- peaks: float32 [64], replicated
The draws below stay inside these ranges and needn't reach their ends.
Inputs may be any that keep to these rules, and one draw needn't show every extreme that they name: `image_of`: tokens come in aligned groups of 4 of one image; an image's tokens are consecutive and lie within one aligned block of 512 rows; numbers never fall along the rows; the last block's last group of 4 is an image of its own. Padding fills whole groups of 4 at the end of each aligned block of 512 rows, at most half of the block; the first group of every block is live and the last block has none; a padding token carries the image number of the token before it. `request_of`: -1 exactly on merged rows of padding; on the other rows request numbers never fall along the rows, and every request has some row.
All inputs are finite; a program needn't handle non-finite values.
Results may differ from the reference program's by a relative error of at most 0.012.
The reference program's roundings to bfloat16 on the way (of `normed`, `qkv`, `weights`, `attended`, `normed2` and `merged`) count: a program that leaves them out, or rounds other values in their place, can miss the bound.
Values may be sent and summed in bfloat16 or wider, within the bound.
A program may use at most 192 MiB of HBM per device.

```python
import jax
import jax.numpy as jnp
from jax import lax

D = 1408
HEADS = 16
OUT = 4096
TOK_DEV = 512
TOKENS = 65536
REQUESTS = 64


def layout(key):
    devices = TOKENS // TOK_DEV
    groups = TOK_DEV // 4
    key_live = jax.random.fold_in(key, 11)
    key_cut = jax.random.fold_in(key, 23)
    device_index = jnp.arange(devices, dtype=jnp.int32)[:, None]
    live_count = jax.random.randint(key_live, (devices, 1), groups // 2, groups + 1)
    live_count = jnp.where(device_index == devices - 1, groups, live_count)
    index = jnp.arange(groups, dtype=jnp.int32)[None, :]
    alive = (index < live_count).astype(jnp.int32)
    starts = (jax.random.randint(key_cut, (devices, groups), 0, 8) == 0).astype(jnp.int32)
    starts = jnp.where(index == 0, 1, starts * alive)
    starts = jnp.where((device_index == devices - 1) & (index == groups - 1), 1, starts)
    positions = jnp.where(starts == 1, index, -1)
    opened = jax.lax.cummax(positions, axis=1)
    image = device_index * groups + opened
    flat_alive = alive.reshape(-1)
    order = jnp.cumsum(flat_alive) - 1
    total = jnp.sum(flat_alive)
    request = jnp.where(flat_alive == 1, order * REQUESTS // total, -1)
    return (image.reshape(-1).astype(jnp.int32), flat_alive.astype(jnp.int32), request.astype(jnp.int32))


def draw_image_of(key, part):
    image, alive, request = layout(key)
    return jnp.repeat(image, 4, total_repeat_length=TOKENS)


def draw_live(key, part):
    image, alive, request = layout(key)
    return jnp.repeat(alive, 4, total_repeat_length=TOKENS)


def draw_request_of(key, part):
    image, alive, request = layout(key)
    return request


def draw_w_qkv(key, part):
    base = jax.random.normal(key, (D, 3 * D), jnp.float32) * D ** (-0.5)
    return base.astype(jnp.bfloat16)


def levels(key, shape, split, smallest, largest):
    loudness, own = 1.0, jax.random.fold_in(key, 6)
    for dim, shards_of in split:
        steps = jnp.exp(jax.random.uniform(jax.random.fold_in(own, dim), (shards_of,), jnp.float32, smallest / len(split), largest / len(split)))
        loudness = loudness * jnp.repeat(steps, shape[dim] // shards_of).reshape([-1 if axis == dim else 1 for axis in range(len(shape))])
    return loudness


def scatter_about(rng, extent, scale, reach, pieces=(), kind=jnp.bfloat16):
    drawn = jax.random.normal(rng, extent, jnp.float32) * scale
    if len(pieces) > 0:
        drawn = levels(rng, extent, pieces, -0.22, 0.18) * drawn
    return jnp.clip(drawn, min=-reach, max=reach).astype(kind)


def setup_inputs(seed: int = 0) -> dict:
    keys = jax.random.split(jax.random.key(seed), 15)
    return {
        "tokens": scatter_about(keys[0], (TOKENS, D), 1.0, 6.0, ((0, 128),)),
        "image_of": draw_image_of(jax.random.fold_in(keys[14], 71), 0),
        "live": draw_live(jax.random.fold_in(keys[14], 71), 0),
        "request_of": draw_request_of(jax.random.fold_in(keys[14], 71), 0),
        "ln1_gain": jnp.clip(1.0 + 0.1 * jax.random.normal(keys[4], (D,), jnp.float32), 0.5, 1.5),
        "ln1_shift": scatter_about(keys[5], (D,), 0.5, 3.0, (), jnp.float32),
        "w_qkv": draw_w_qkv(jax.random.fold_in(keys[14], 71), 0),
        "b_qkv": scatter_about(keys[7], (3 * D,), 0.5, 3.0, (), jnp.float32),
        "w_out": scatter_about(keys[8], (D, D), D ** -0.5, 0.15625, ((0, 16),)),
        "b_out": scatter_about(keys[9], (D,), 0.5, 3.0, (), jnp.float32),
        "ln2_gain": jnp.clip(1.0 + 0.1 * jax.random.normal(keys[10], (D,), jnp.float32), 0.5, 1.5),
        "ln2_shift": scatter_about(keys[11], (D,), 0.5, 3.0, (), jnp.float32),
        "w_proj": scatter_about(keys[12], (4 * D, OUT), (4 * D) ** -0.5, 0.078125, ((1, 16),)),
        "b_proj": scatter_about(keys[13], (OUT,), 0.5, 3.0, ((0, 16),), jnp.float32),
    }


def layer_norm(values, gain, shift):
    mean_value = lax.optimization_barrier(jnp.mean(values, axis=-1, keepdims=True))
    centred = values - mean_value
    variance = lax.optimization_barrier(jnp.mean(centred * centred, axis=-1, keepdims=True))
    return centred * lax.rsqrt(variance + 1e-06) * gain + shift

def reference(tokens, image_of, live, request_of, ln1_gain, ln1_shift, w_qkv, b_qkv, w_out, b_out, ln2_gain, ln2_shift, w_proj, b_proj):
    devices = TOKENS // TOK_DEV
    head_size = D // HEADS
    scale = head_size ** (-0.5)

    def per_device(items):
        block_tokens, block_images, block_live = items
        resid = block_tokens.astype(jnp.float32)
        normed = layer_norm(resid, ln1_gain, ln1_shift).astype(jnp.bfloat16)
        qkv = (jnp.dot(normed, w_qkv, preferred_element_type=jnp.float32) + b_qkv).astype(jnp.bfloat16)
        queries = qkv[:, :D].reshape(TOK_DEV, HEADS, head_size).astype(jnp.float32)
        keys_all = qkv[:, D:2 * D].reshape(TOK_DEV, HEADS, head_size).astype(jnp.float32)
        values_all = qkv[:, 2 * D:].reshape(TOK_DEV, HEADS, head_size).astype(jnp.float32)
        scores = jnp.einsum('qhe,khe->hqk', queries, keys_all) * scale
        allowed = (block_images[:, None] == block_images[None, :]) & (block_live[None, :] == 1)
        scores = jnp.where(allowed[None], scores, jnp.float32(-1e+30))
        top = lax.optimization_barrier(jnp.max(scores, axis=-1, keepdims=True))
        expo = jnp.exp(scores - top)
        weights = (expo / lax.optimization_barrier(jnp.sum(expo, axis=-1, keepdims=True))).astype(jnp.bfloat16)
        attended = jnp.einsum('hqk,khe->qhe', weights.astype(jnp.float32), values_all)
        attended = attended.reshape(TOK_DEV, D).astype(jnp.bfloat16)
        resid = resid + (jnp.dot(attended, w_out, preferred_element_type=jnp.float32) + b_out)
        normed2 = layer_norm(resid, ln2_gain, ln2_shift).astype(jnp.bfloat16)
        return normed2.reshape(TOK_DEV // 4, 4 * D)
    merged = lax.map(per_device, (tokens.reshape(devices, TOK_DEV, D), image_of.reshape(devices, TOK_DEV), live.reshape(devices, TOK_DEV)))
    merged = merged.reshape(TOKENS // 4, 4 * D)
    projected = jnp.dot(merged, w_proj, preferred_element_type=jnp.float32) + b_proj
    labels = jnp.arange(REQUESTS, dtype=jnp.int32)
    member = request_of[:, None] == labels[None, :]
    row_squares = lax.optimization_barrier(jnp.sum(projected * projected, axis=1))
    row_top = lax.optimization_barrier(jnp.max(projected, axis=1))
    sumsq = lax.optimization_barrier(jnp.sum(jnp.where(member, row_squares[:, None], jnp.float32(0.0)), axis=0))
    entries = lax.optimization_barrier(jnp.sum(member.astype(jnp.float32), axis=0)) * jnp.float32(OUT)
    top = lax.optimization_barrier(jnp.max(jnp.where(member, row_top[:, None], jnp.float32(-jnp.inf)), axis=0))
    rms = jnp.sqrt(sumsq / entries + 1e-06)
    valid = request_of >= 0
    safe_ids = jnp.where(valid, request_of, 0).astype(jnp.int32)
    row_rms = rms[safe_ids]
    features = jnp.where(valid[:, None], projected / row_rms[:, None], jnp.float32(0.0)).astype(jnp.bfloat16)
    peaks = top / rms
    return (features, peaks)
```

```python
import functools

import jax
import jax.numpy as jnp
from jax import lax
from jax.experimental import pallas as pl
from jax.experimental.pallas import tpu as pltpu
from jax.sharding import PartitionSpec as P

HEADS = 16
REQUESTS = 64
MESH = pl.DeviceIdType.MESH


def normalize(values, gain, shift):
    mean_value = jnp.mean(values, axis=-1, keepdims=True)
    centred = values - mean_value
    variance = jnp.mean(centred * centred, axis=-1, keepdims=True)
    return centred * lax.rsqrt(variance + 1e-06) * gain + shift


def attention(qkv, image_ids, live_flags, heads):
    count_rows = qkv.shape[0]
    width = qkv.shape[1] // 3
    head_size = width // heads
    scale = head_size ** (-0.5)
    queries = qkv[:, :width].reshape(count_rows, heads, head_size)
    keys_all = qkv[:, width : 2 * width].reshape(count_rows, heads, head_size)
    values_all = qkv[:, 2 * width :].reshape(count_rows, heads, head_size)
    key_live = live_flags[None, :] == 1
    scores = jnp.einsum("qhe,khe->hqk", queries, keys_all, preferred_element_type=jnp.float32) * scale
    allowed = (image_ids[:, None] == image_ids[None, :]) & key_live
    scores = jnp.where(allowed[None], scores, jnp.float32(-1e30))
    top = jnp.max(scores, axis=-1, keepdims=True)
    expo = jnp.exp(scores - top)
    weights = (expo / jnp.sum(expo, axis=-1, keepdims=True)).astype(jnp.bfloat16)
    mixed = jnp.einsum("hqk,khe->qhe", weights, values_all, preferred_element_type=jnp.float32)
    return mixed.reshape(count_rows, width).astype(jnp.bfloat16)


class Copies:
    def __init__(self, send_sems, recv_sems, local_sems):
        self.send_sems, self.recv_sems, self.local_sems = send_sems, recv_sems, local_sems
        self.remote_count = 0
        self.local_count = 0
        self.sent = []

    def remote(self, src, dst, to):
        index = self.remote_count
        self.remote_count += 1
        copy = pltpu.make_async_remote_copy(
            src_ref=src,
            dst_ref=dst,
            send_sem=self.send_sems.at[index],
            recv_sem=self.recv_sems.at[index],
            device_id=to,
            device_id_type=MESH,
        )
        copy.start()
        self.sent.append(copy)
        return copy

    def local(self, src, dst):
        index = self.local_count
        self.local_count += 1
        copy = pltpu.make_async_copy(src, dst, self.local_sems.at[index])
        copy.start()
        return copy


def column_of(row):
    n = row.shape[1]
    wide = jnp.broadcast_to(row, (n, n))
    diagonal = lax.broadcasted_iota(jnp.int32, (n, n), 0) == lax.broadcasted_iota(jnp.int32, (n, n), 1)
    return jnp.sum(jnp.where(diagonal, wide, 0), axis=1, keepdims=True)


def project_kernel(
    merged_hbm, weight_hbm, bias_hbm, request_ref, out_hbm, stats_ref,
    mbuf, wbuf, bbuf, stage, squares, tops, first, second,
    send_sems, recv_sems, local_sems,
):
    d, f = lax.axis_index("dp"), lax.axis_index("fsdp")
    z, y = f // 4, f % 4
    core = d % 2
    partner = (d + 1 - 2 * core, f)

    def at_y(step):
        return (d, z * 4 + (y + step + 4) % 4)

    def at_z(step):
        return (d, ((z + step + 4) % 4) * 4 + y)

    barrier = pltpu.get_barrier_semaphore()
    for step in range(1, 16):
        pl.semaphore_signal(barrier, inc=1, device_id=(d, (f + step) % 16), device_id_type=MESH)
    for step in range(1, 8):
        pl.semaphore_signal(barrier, inc=1, device_id=((d + step) % 8, f), device_id_type=MESH)
    copies = Copies(send_sems, recv_sems, local_sems)
    loads = [copies.local(weight_hbm, wbuf.at[0]), copies.local(merged_hbm, mbuf.at[0]), copies.local(bias_hbm, bbuf.at[0])]
    pl.semaphore_wait(barrier, 22)

    own = [2 * core, 2 * core + 1]
    w_right = [copies.remote(weight_hbm.at[own[k]], wbuf.at[3, own[k]], at_y(1)) for k in (0, 1)]
    w_left = [copies.remote(weight_hbm.at[own[k]], wbuf.at[1, own[k]], at_y(-1)) for k in (1, 0)][::-1]
    m_up = [copies.remote(merged_hbm.at[s], mbuf.at[3, s], at_z(1)) for s in (0, 1, 2, 3)]
    m_down = {s: copies.remote(merged_hbm.at[s], mbuf.at[1, s], at_z(-1)) for s in (2, 3, 0, 1)}
    b_all = {r: copies.remote(bias_hbm, bbuf.at[4 - r], at_y(r)) for r in (1, 2, 3)}
    for load in loads:
        load.wait()

    lane = lax.broadcasted_iota(jnp.int32, (128, 128), 1)

    def block(rz, ry):
        total = jnp.dot(mbuf[rz, 0], wbuf[ry, 0], preferred_element_type=jnp.float32)
        for s in range(1, 4):
            total += jnp.dot(mbuf[rz, s], wbuf[ry, s], preferred_element_type=jnp.float32)
        total += bbuf[ry]
        stage[rz, ry] = total.astype(jnp.bfloat16)
        left, right = total[:, :128], total[:, 128:]
        return left * left + right * right, jnp.maximum(left, right)

    outs, stored = [], []

    def first_block(rz, ry):
        squares[rz], tops[rz] = block(rz, ry)

    def more_block(rz, ry):
        square, top = block(rz, ry)
        squares[rz] = squares[rz] + square
        tops[rz] = jnp.maximum(tops[rz], top)

    def hand_over(rz, ry):
        row_block = ((z + rz) % 4) * 4 + y
        if ry == 0:
            stored.append(copies.local(stage.at[rz, ry], out_hbm.at[row_block]))
        else:
            outs.append(copies.remote(stage.at[rz, ry], out_hbm.at[row_block], at_y(ry)))

    first_block(0, 0)
    hand_over(0, 0)

    m_fwd = []
    for k in (0, 1):
        m_up[k].wait_recv()
        m_fwd.append(copies.remote(mbuf.at[3, k], mbuf.at[2, k], at_z(1)))
        m_down[2 + k].wait_recv()
        m_fwd.append(copies.remote(mbuf.at[1, 2 + k], mbuf.at[2, 2 + k], at_z(-1)))
    w_fwd, swap = [], []
    w_right[0].wait_recv()
    w_fwd.append(copies.remote(wbuf.at[3, own[0]], wbuf.at[2, own[0]], at_y(1)))
    swap.append(copies.remote(wbuf.at[3, own[0]], wbuf.at[3, own[0]], partner))
    w_left[1].wait_recv()
    w_fwd.append(copies.remote(wbuf.at[1, own[1]], wbuf.at[2, own[1]], at_y(-1)))
    swap.append(copies.remote(wbuf.at[1, own[1]], wbuf.at[1, own[1]], partner))
    for copy in (m_up[2], m_up[3], m_down[0], m_down[1]):
        copy.wait_recv()
    for rz in (1, 3):
        first_block(rz, 0)
        hand_over(rz, 0)
    w_right[1].wait_recv()
    swap.append(copies.remote(wbuf.at[3, own[1]], wbuf.at[3, own[1]], partner))
    w_left[0].wait_recv()
    swap.append(copies.remote(wbuf.at[1, own[0]], wbuf.at[1, own[0]], partner))
    for copy in swap + list(b_all.values()):
        copy.wait_recv()
    for ry in (1, 3):
        for rz in (0, 1, 3):
            more_block(rz, ry)
            hand_over(rz, ry)
    for copy in m_fwd:
        copy.wait_recv()
    first_block(2, 0)
    hand_over(2, 0)
    for ry in (1, 3):
        more_block(2, ry)
        hand_over(2, ry)
    swap = []
    for k in (0, 1):
        w_fwd[k].wait_recv()
        swap.append(copies.remote(wbuf.at[2, own[k]], wbuf.at[2, own[k]], partner))
    for copy in swap:
        copy.wait_recv()
    for rz in range(4):
        more_block(rz, 2)
        hand_over(rz, 2)

    sums = jnp.zeros((1, 128), jnp.float32)
    entries = jnp.zeros((1, 128), jnp.float32)
    peak = jnp.full((1, 128), -jnp.inf, jnp.float32)
    for rz in range(4):
        row_block = ((z + rz) % 4) * 4 + y
        member = column_of(request_ref[pl.ds(row_block, 1), :]) == lane
        row_square = jnp.sum(squares[rz], axis=1, keepdims=True)
        row_top = jnp.max(tops[rz], axis=1, keepdims=True)
        sums += jnp.sum(jnp.where(member, row_square, 0.0), axis=0, keepdims=True)
        entries += jnp.sum(jnp.where(member, 1024.0, 0.0), axis=0, keepdims=True)
        peak = jnp.maximum(peak, jnp.max(jnp.where(member, row_top, -jnp.inf), axis=0, keepdims=True))

    def pack(sums, entries, peak):
        return jnp.concatenate([sums, entries, peak, jnp.zeros((5, 128), jnp.float32)], axis=0)

    def combine(slots, count):
        total, high = slots[0], slots[0]
        for i in range(1, count):
            total = total + slots[i]
            high = jnp.maximum(high, slots[i])
        return total[0:1], total[1:2], high[2:3]

    first[f] = pack(sums, entries, peak)
    round_one = [copies.remote(first.at[f], first.at[f], (d, (f + step) % 16)) for step in range(1, 16)]
    for copy in round_one:
        copy.wait_recv()
    second[d] = pack(*combine(first, 16))
    round_two = [copies.remote(second.at[d], second.at[d], ((d + step) % 8, f)) for step in range(1, 8)]
    for copy in round_two:
        copy.wait_recv()
    sums, entries, peak = combine(second, 8)
    lanes = lax.broadcasted_iota(jnp.int32, (1, 128), 1)
    rms = jnp.sqrt(sums / jnp.where(lanes < REQUESTS, entries, 1.0) + 1e-06)
    stats_ref[...] = pack(rms, peak / rms, peak)

    for copy in outs:
        copy.wait_recv()
    for copy in stored:
        copy.wait()
    for copy in copies.sent:
        copy.wait_send()


def project(merged, w_proj, b_proj, request_of):
    depth = merged.shape[2]
    any_space = pl.BlockSpec(memory_space=pl.ANY)
    vmem = pl.BlockSpec(memory_space=pltpu.VMEM)
    return pl.pallas_call(
        project_kernel,
        out_shape=(
            jax.ShapeDtypeStruct((16, 128, 256), jnp.bfloat16),
            jax.ShapeDtypeStruct((8, 128), jnp.float32),
        ),
        in_specs=[any_space, any_space, any_space, vmem],
        out_specs=(any_space, vmem),
        scratch_shapes=[
            pltpu.VMEM((4, 4, 128, depth), jnp.bfloat16),
            pltpu.VMEM((4, 4, depth, 256), jnp.bfloat16),
            pltpu.VMEM((4, 1, 256), jnp.float32),
            pltpu.VMEM((4, 4, 128, 256), jnp.bfloat16),
            pltpu.VMEM((4, 128, 128), jnp.float32),
            pltpu.VMEM((4, 128, 128), jnp.float32),
            pltpu.VMEM((16, 8, 128), jnp.float32),
            pltpu.VMEM((8, 8, 128), jnp.float32),
            pltpu.SemaphoreType.DMA((61,)),
            pltpu.SemaphoreType.DMA((61,)),
            pltpu.SemaphoreType.DMA((7,)),
        ],
        compiler_params=pltpu.CompilerParams(
            collective_id=0, has_side_effects=True, vmem_limit_bytes=60 * 1024 * 1024
        ),
        name="project",
    )(merged, w_proj.reshape(4, depth, 256), b_proj.reshape(1, 256), request_of.reshape(16, 128))


def shards(
    tokens, image_of, live, request_of, ln1_gain, ln1_shift, w_qkv, b_qkv,
    w_out, b_out, ln2_gain, ln2_shift, w_proj, b_proj,
):
    count_rows, width = tokens.shape
    resid = tokens.astype(jnp.float32)
    normed = normalize(resid, ln1_gain, ln1_shift).astype(jnp.bfloat16)
    mixed = jnp.dot(normed, lax.all_gather(w_qkv, "fsdp", axis=0, tiled=True), preferred_element_type=jnp.float32)
    qkv = (mixed + b_qkv).astype(jnp.bfloat16)
    attended = attention(qkv, image_of, live, HEADS)
    projected_out = jnp.dot(
        attended, lax.all_gather(w_out, "fsdp", axis=0, tiled=True), preferred_element_type=jnp.float32
    )
    resid = resid + (projected_out + b_out)
    normed2 = normalize(resid, ln2_gain, ln2_shift).astype(jnp.bfloat16)
    merged = normed2.reshape(count_rows // 4, 4, width).transpose(1, 0, 2)
    raw, stats = project(merged, w_proj, b_proj, request_of)
    rms, peaks = stats[0, :REQUESTS], stats[1, :REQUESTS]
    labels = jnp.arange(REQUESTS, dtype=jnp.int32)
    member = request_of[:, None] == labels[None, :]
    valid = request_of >= 0
    row_rms = jnp.sum(jnp.where(member, rms[None, :], 0.0), axis=1) + jnp.where(valid, 0.0, 1.0)
    projected = raw.reshape(raw.shape[0] * raw.shape[1], raw.shape[2]).astype(jnp.float32)
    features = jnp.where(valid[:, None], projected / row_rms[:, None], 0.0).astype(jnp.bfloat16)
    return (features, peaks)


def solution(mesh):
    return jax.shard_map(
        shards,
        mesh=mesh,
        in_specs=(
            P(("dp", "fsdp"), None),
            P(("dp", "fsdp")),
            P(("dp", "fsdp")),
            P("dp"),
            P(),
            P(),
            P("fsdp", None),
            P(),
            P("fsdp", None),
            P(),
            P(),
            P(),
            P(None, "fsdp"),
            P("fsdp"),
        ),
        out_specs=(P("dp", "fsdp"), P()),
        check_vma=False,
    )
```
